32 devices in a mesh: dp: 2 (over y), seq: 4 (over z), chan: 4 (over x, core).
Axes of the slice: x: 2, y: 2, z: 4, core: 2. Of those that a mesh axis runs over, the one named last changes fastest.
Arguments:
- tokens: bfloat16 [16384, 1024], P(('dp', 'seq'), 'chan'), may hold values from -6 to 6
- gain_one: bfloat16 [1024], P('chan'), may hold values from 0.25 to 1.75
- in_weight: bfloat16 [1024, 3, 1024], P(None, None, 'chan'), may hold values from -0.1875 to 0.1875
- conv_weight: bfloat16 [3, 1024], P(None, 'chan'), may hold values from -3 to 3
- out_weight: bfloat16 [1024, 1024], P('chan'), may hold values from -0.1875 to 0.1875
- gain_two: bfloat16 [1024], replicated, may hold values from 0.25 to 1.75
- gate_up_weight: bfloat16 [1024, 2, 4608], P(None, None, 'chan'), may hold values from -0.1875 to 0.1875
- down_weight: bfloat16 [4608, 1024], P('chan'), may hold values from -0.09375 to 0.09375
- cotangent: bfloat16 [16384, 1024], P(('dp', 'seq'), 'chan'), may hold values from -6 to 6
Outputs:
- result: bfloat16 [16384, 1024], P(('dp', 'seq'), 'chan')
- grad_tokens: bfloat16 [16384, 1024], P(('dp', 'seq'), 'chan')
- grad_gain_one: float32 [1024], P('chan')
- grad_in_weight: float32 [1024, 3, 1024], P(None, None, 'chan')
- grad_conv_weight: float32 [3, 1024], P(None, 'chan')
- grad_out_weight: float32 [1024, 1024], P('chan')
- grad_gain_two: float32 [1024], P('chan')
- grad_gate_up: float32 [1024, 2, 4608], P(None, None, 'chan')
- grad_down: float32 [4608, 1024], P('chan')
The draws below stay inside these ranges and needn't reach their ends.
All inputs are finite; a program needn't handle non-finite values.
Results may differ from the reference program's by a relative error of at most 0.018.
Values may be sent and summed in bfloat16 or wider, within the bound.
No kernel may reach another device: no remote copies, remote signals or barrier semaphores. Data moves between devices by JAX's collectives and lax.ppermute only.
A program may use at most 256 MiB of HBM per device.

```python
import jax
import jax.numpy as jnp
from jax import lax

D = 1024
FF = 4608
TOK_DEV = 2048
TOKENS = 16384
N_DP = 2
N_SEQ = 4


def steps_of(rng, shape, pieces, low, top_value):
    def one(position, parts):
        heights = jax.random.uniform(jax.random.fold_in(jax.random.fold_in(rng, 6), position), (parts,), jnp.float32, low / len(pieces), top_value / len(pieces))
        return jnp.repeat(jnp.exp(heights), shape[position] // parts).reshape((-1,) + (1,) * (len(shape) - position - 1))

    level = one(*pieces[0])
    for cut in pieces[1:]:
        level = level * one(*cut)
    return level


def normal_values(key, extent, deviation, limit, pieces=(), held_as=jnp.bfloat16):
    drawn = deviation * jax.random.normal(key, extent, jnp.float32)
    if pieces:
        drawn = drawn * steps_of(key, extent, pieces, -0.22, 0.18)
    return jnp.clip(drawn, -limit, limit).astype(held_as)


def setup_inputs(seed: int = 0) -> dict:
    seeds = jax.random.split(jax.random.key(seed), 10)
    return {
        "tokens": normal_values(seeds[0], (TOKENS, D), 1.0, 6.0, ((0, 8), (1, 4))),
        "gain_one": jnp.clip(1.0 + 0.15 * jax.random.normal(seeds[1], (D,), jnp.float32), 0.25, 1.75).astype(jnp.bfloat16),
        "in_weight": normal_values(seeds[2], (D, 3, D), D ** -0.5, 0.1875, ((2, 4),)),
        "conv_weight": normal_values(seeds[3], (3, D), 0.7, 3.0, ((1, 4),)),
        "out_weight": normal_values(seeds[4], (D, D), D ** -0.5, 0.1875, ((0, 4),)),
        "gain_two": jnp.clip(1.0 + 0.15 * jax.random.normal(seeds[5], (D,), jnp.float32), 0.25, 1.75).astype(jnp.bfloat16),
        "gate_up_weight": normal_values(seeds[6], (D, 2, FF), D ** -0.5, 0.1875, ((2, 4),)),
        "down_weight": normal_values(seeds[7], (FF, D), FF ** -0.5, 0.09375, ((0, 4),)),
        "cotangent": normal_values(seeds[8], (TOKENS, D), 1.0, 6.0, ((0, 8), (1, 4))),
    }


epsilon = 1e-05

def block_forward(token_block, state, weights):
    gain_one, in_flat, kernel, out_weight, gain_two, gu_flat, down_weight = weights
    count = token_block.shape[0]
    x_float = token_block.astype(jnp.float32)
    inv_one = lax.rsqrt(lax.optimization_barrier(jnp.mean(x_float * x_float, axis=-1, keepdims=True)) + epsilon)
    normed_one = (x_float * inv_one * gain_one).astype(jnp.bfloat16)
    projected = jnp.dot(normed_one, in_flat, preferred_element_type=jnp.float32)
    gate_b = projected[:, :D]
    gate_c = projected[:, D:2 * D]
    values = projected[:, 2 * D:]
    product = gate_b * values
    extended = jnp.concatenate([state, product], axis=0)
    conv_out = kernel[0] * extended[0:count] + kernel[1] * extended[1:count + 1] + kernel[2] * extended[2:count + 2]
    mixed = (gate_c * conv_out).astype(jnp.bfloat16)
    resid = x_float + jnp.dot(mixed, out_weight, preferred_element_type=jnp.float32)
    inv_two = lax.rsqrt(lax.optimization_barrier(jnp.mean(resid * resid, axis=-1, keepdims=True)) + epsilon)
    normed_two = (resid * inv_two * gain_two).astype(jnp.bfloat16)
    gate_up = jnp.dot(normed_two, gu_flat, preferred_element_type=jnp.float32)
    gate_pre = gate_up[:, :FF]
    up_pre = gate_up[:, FF:]
    sigma = jax.nn.sigmoid(gate_pre)
    hidden = (gate_pre * sigma * up_pre).astype(jnp.bfloat16)
    output = (resid + jnp.dot(hidden, down_weight, preferred_element_type=jnp.float32)).astype(jnp.bfloat16)
    return (x_float, inv_one, normed_one, gate_b, gate_c, values, extended, conv_out, mixed, resid, inv_two, normed_two, gate_pre, up_pre, sigma, hidden, output)

def block_backward(token_block, state, next_grad, cot_block, weights):
    gain_one, in_flat, kernel, out_weight, gain_two, gu_flat, down_weight = weights
    x_float, inv_one, normed_one, gate_b, gate_c, values, extended, conv_out, mixed, resid, inv_two, normed_two, gate_pre, up_pre, sigma, hidden, output = block_forward(token_block, state, weights)
    count = token_block.shape[0]
    cot_float = cot_block.astype(jnp.float32)
    d_hidden = jnp.dot(cot_block, down_weight.T, preferred_element_type=jnp.float32)
    grad_down = jnp.dot(hidden.T, cot_block, preferred_element_type=jnp.float32)
    d_gate = d_hidden * up_pre * sigma * (1.0 + gate_pre * (1.0 - sigma))
    d_up = d_hidden * gate_pre * sigma
    d_gate_up = jnp.concatenate([d_gate, d_up], axis=1).astype(jnp.bfloat16)
    grad_gate_up = jnp.dot(normed_two.T, d_gate_up, preferred_element_type=jnp.float32)
    d_norm_two = jnp.dot(d_gate_up, gu_flat.T, preferred_element_type=jnp.float32)
    scaled_two = resid * inv_two
    grad_gain_two = lax.optimization_barrier(jnp.sum(d_norm_two * scaled_two, axis=0))
    pulled_two = d_norm_two * gain_two
    d_resid = cot_float + inv_two * (pulled_two - scaled_two * lax.optimization_barrier(jnp.mean(pulled_two * scaled_two, axis=-1, keepdims=True)))
    d_out = d_resid.astype(jnp.bfloat16)
    d_mixed = jnp.dot(d_out, out_weight.T, preferred_element_type=jnp.float32)
    grad_out = jnp.dot(mixed.T, d_out, preferred_element_type=jnp.float32)
    d_gate_c = d_mixed * conv_out
    d_conv = d_mixed * gate_c
    grad_ext = jnp.concatenate([d_conv, next_grad], axis=0)
    d_product = kernel[2] * grad_ext[0:count] + kernel[1] * grad_ext[1:count + 1] + kernel[0] * grad_ext[2:count + 2]
    grad_conv = jnp.stack([lax.optimization_barrier(jnp.sum(d_conv * extended[shift_index:shift_index + count], axis=0)) for shift_index in range(3)])
    d_project = jnp.concatenate([d_product * values, d_gate_c, d_product * gate_b], axis=1).astype(jnp.bfloat16)
    grad_in = jnp.dot(normed_one.T, d_project, preferred_element_type=jnp.float32)
    d_norm_one = jnp.dot(d_project, in_flat.T, preferred_element_type=jnp.float32)
    scaled_one = x_float * inv_one
    grad_gain_one = lax.optimization_barrier(jnp.sum(d_norm_one * scaled_one, axis=0))
    pulled_one = d_norm_one * gain_one
    d_tokens = d_resid + inv_one * (pulled_one - scaled_one * lax.optimization_barrier(jnp.mean(pulled_one * scaled_one, axis=-1, keepdims=True)))
    grads = (grad_gain_one, grad_in, grad_conv, grad_out, grad_gain_two, grad_gate_up, grad_down)
    return (d_conv[0:2], d_tokens.astype(jnp.bfloat16), grads)

def add_pair(first, second):
    return first + second

def reference(tokens, gain_one, in_weight, conv_weight, out_weight, gain_two, gate_up_weight, down_weight, cotangent):
    weights = (gain_one.astype(jnp.float32), in_weight.reshape(D, 3 * D), conv_weight.astype(jnp.float32), out_weight, gain_two.astype(jnp.float32), gate_up_weight.reshape(D, 2 * FF), down_weight)
    blocks = N_DP * N_SEQ
    token_blocks = tokens.reshape(blocks, TOK_DEV, D)
    cot_blocks = cotangent.reshape(blocks, TOK_DEV, D)
    block_ids = jnp.arange(blocks, dtype=jnp.int32)
    zero_state = jnp.zeros((2, D), jnp.float32)

    def forward_step(carry_state, inputs):
        token_block, block_id = inputs
        state = jnp.where(block_id % N_SEQ == 0, zero_state, carry_state)
        saved = block_forward(token_block, state, weights)
        return (saved[6][TOK_DEV:], (state, saved[-1]))
    last_state, (states, outputs) = lax.scan(forward_step, zero_state, (token_blocks, block_ids))
    zero_grads = (jnp.zeros((D,), jnp.float32), jnp.zeros((D, 3 * D), jnp.float32), jnp.zeros((3, D), jnp.float32), jnp.zeros((D, D), jnp.float32), jnp.zeros((D,), jnp.float32), jnp.zeros((D, 2 * FF), jnp.float32), jnp.zeros((FF, D), jnp.float32))

    def backward_step(carry, inputs):
        next_grad, grads = carry
        token_block, cot_block, state, block_id = inputs
        next_grad = jnp.where(block_id % N_SEQ == N_SEQ - 1, zero_state, next_grad)
        first_rows, d_tokens, block_grads = block_backward(token_block, state, next_grad, cot_block, weights)
        grads = jax.tree.map(add_pair, grads, block_grads)
        return ((first_rows, grads), d_tokens)
    final_carry, d_blocks = lax.scan(backward_step, (zero_state, zero_grads), (token_blocks, cot_blocks, states, block_ids), reverse=True)
    grads = final_carry[1]
    return (outputs.reshape(TOKENS, D), d_blocks.reshape(TOKENS, D), grads[0], grads[1].reshape(D, 3, D), grads[2], grads[3], grads[4], grads[5].reshape(D, 2, FF), grads[6])
```

```python
import jax
import jax.numpy as jnp
from jax import lax
from jax.sharding import PartitionSpec as P

epsilon = 1e-05
chunks = 2
f32 = jnp.float32
bf16 = jnp.bfloat16


def dot(a, b):
    return jnp.dot(a, b, preferred_element_type=f32)


def dot_t(a, b):
    return lax.dot_general(a, b, (((1,), (1,)), ((), ())), preferred_element_type=f32)


def t_dot(a, b):
    return lax.dot_general(a, b, (((0,), (0,)), ((), ())), preferred_element_type=f32)


def after(value, *deps):
    return lax.optimization_barrier((value, *deps))[0]


def shifted(value, axis, by):
    length = lax.axis_size(axis)
    pairs = [(i, i + by) for i in range(length) if 0 <= i + by < length]
    return lax.ppermute(value, axis, pairs)


def swap(value, axis, bit):
    return lax.ppermute(value, axis, [(i, i ^ bit) for i in range(lax.axis_size(axis))])


def bits_of(axis):
    size = lax.axis_size(axis)
    bits = []
    while (1 << len(bits)) < size:
        bits.append(1 << len(bits))
    return bits


def order_of(bits):
    if not bits:
        return [0]
    rest = order_of(bits[1:])
    return [r | bits[0] for r in rest] + rest


def gather(own):
    pieces = {0: own}
    for bit in reversed(bits_of("chan")):
        for r in list(pieces):
            pieces[r ^ bit] = swap(pieces[r], "chan", bit)
    return jnp.concatenate([pieces[r] for r in order_of(bits_of("chan"))], axis=1)


def scatter(product):
    size = lax.axis_size("chan")
    bits = bits_of("chan")
    lo, half = 0, size // 2
    keep = None
    for bit in bits:
        if keep is None:
            sent = product(0, half).astype(bf16)
            keep = product(half, size)
        else:
            width = keep.shape[1] // 2
            sent, keep = keep[:, :width].astype(bf16), keep[:, width:]
        keep = keep + swap(sent, "chan", bit).astype(f32)
    return keep


def total(value, axis="chan"):
    size = lax.axis_size(axis)
    out = value
    for r in range(1, size):
        out = out + swap(value, axis, r)
    return out


def reduce_line(value, axis):
    size = lax.axis_size(axis)
    half = size // 2
    for step in range(half - 1):
        got = lax.ppermute(value, axis, [(step, step + 1), (size - 1 - step, size - 2 - step)])
        value = (value.astype(f32) + got.astype(f32)).astype(bf16)
    got = lax.ppermute(value, axis, [(half - 1, half), (half, half - 1)])
    value = (value.astype(f32) + got.astype(f32)).astype(bf16)
    index = lax.axis_index(axis)
    for step in reversed(range(half - 1)):
        got = lax.ppermute(value, axis, [(step + 1, step), (size - 2 - step, size - 1 - step)])
        value = jnp.where((index == step) | (index == size - 1 - step), got, value)
    return value


def reduce_grad(value):
    rows = value.shape[0] // 2
    me = lax.axis_index("dp")
    other = lax.dynamic_slice_in_dim(value, (1 - me) * rows, rows, 0)
    mine = lax.dynamic_slice_in_dim(value, me * rows, rows, 0)
    got = swap(other, "dp", 1)
    mine = (mine.astype(f32) + got.astype(f32)).astype(bf16)
    mine = reduce_line(mine, "seq")
    got = swap(mine, "dp", 1)
    first = jnp.where(me == 0, mine, got)
    second = jnp.where(me == 0, got, mine)
    return jnp.concatenate([first, second], axis=0).astype(f32)


def shards(
    tokens,
    gain_one,
    in_weight,
    conv_weight,
    out_weight,
    gain_two,
    gate_up_weight,
    down_weight,
    cotangent,
):
    size = lax.axis_size("chan")
    index = lax.axis_index("chan")
    order = order_of(bits_of("chan"))
    place = jnp.array([order.index(r) for r in range(size)], jnp.int32)
    width = in_weight.shape[0]
    local = in_weight.shape[2]
    hidden = gate_up_weight.shape[2]
    count = tokens.shape[0]
    part = count // chunks

    def relative(value, axis):
        return jnp.concatenate(
            [lax.dynamic_slice_in_dim(value, (index ^ r) * local, local, axis) for r in order], axis
        )

    def absolute(value, axis):
        return jnp.concatenate(
            [lax.dynamic_slice_in_dim(value, place[index ^ b] * local, local, axis) for b in range(size)], axis
        )

    w_in = relative(in_weight.reshape(width, 3 * local), 0)
    w_gu = relative(gate_up_weight.reshape(width, 2 * hidden), 0)
    w_out = relative(out_weight, 1)
    w_down = relative(down_weight, 1)
    kernel = conv_weight.astype(f32)
    gain1 = gain_one.astype(f32)
    gain2 = lax.dynamic_slice_in_dim(gain_two, index * local, local, 0).astype(f32)

    def cut(value):
        return [value[k * part : (k + 1) * part] for k in range(chunks)]

    ks = range(chunks)
    x = [v.astype(f32) for v in cut(tokens)]
    cot = [v.astype(f32) for v in cut(cotangent)]

    raw1 = [gather((v * gain1).astype(bf16)) for v in x]
    inv1 = [lax.rsqrt(total(jnp.sum(v * v, axis=1)) / width + epsilon)[:, None] for v in x]
    bcx = [dot(raw1[k], w_in) * inv1[k] for k in ks]
    gate_b = [v[:, :local] for v in bcx]
    gate_c = [v[:, local : 2 * local] for v in bcx]
    values = [v[:, 2 * local :] for v in bcx]
    product = [gate_b[k] * values[k] for k in ks]
    state = shifted(product[-1][part - 2 :], "seq", 1)
    extended = [
        jnp.concatenate([state if k == 0 else product[k - 1][part - 2 :], product[k]], axis=0) for k in ks
    ]
    conv = [
        kernel[0] * e[0:part] + kernel[1] * e[1 : part + 1] + kernel[2] * e[2 : part + 2] for e in extended
    ]
    mixed = [(gate_c[k] * conv[k]).astype(bf16) for k in ks]

    cot_full = [gather(v) for v in cut(cotangent)]

    def columns(a, w):
        block = width // size

        def product(lo, hi):
            return dot(a, w[:, lo * block : hi * block])

        return product

    def columns_t(a, w):
        block = width // size

        def product(lo, hi):
            return dot_t(a, w[lo * block : hi * block])

        return product

    resid = [x[k] + scatter(columns(mixed[k], w_out)) for k in ks]
    raw2 = [gather((v * gain2).astype(bf16)) for v in resid]
    inv2 = [lax.rsqrt(total(jnp.sum(v * v, axis=1)) / width + epsilon)[:, None] for v in resid]

    act, d_gu, inner2, result, d_out_own, d_resid = [], [], [], [], [], []
    gain2_grad = 0.0
    for k in ks:
        gate_up = dot(raw2[k], w_gu) * inv2[k]
        gate = gate_up[:, :hidden]
        up = gate_up[:, hidden:]
        sigma = jax.nn.sigmoid(gate)
        act.append((gate * sigma * up).astype(bf16))
        d_act = dot_t(cot_full[k], w_down)
        d_gate = d_act * up * sigma * (1.0 + gate * (1.0 - sigma))
        d_up = d_act * gate * sigma
        inner2.append(total(jnp.sum(d_gate * gate + d_up * up, axis=1))[:, None])
        d_gu.append((jnp.concatenate([d_gate, d_up], axis=1) * inv2[k]).astype(bf16))
    for k in ks:
        pulled = scatter(columns_t(d_gu[k], w_gu))
        gain2_grad = gain2_grad + jnp.sum(pulled * resid[k], axis=0)
        d_resid.append(
            cot[k] + pulled * gain2 - resid[k] * (inv2[k] * inv2[k] * inner2[k] * (1.0 / width))
        )
        d_out_own.append(d_resid[k].astype(bf16))
    d_out = [gather(v) for v in d_out_own]
    for k in ks:
        result.append((resid[k] + scatter(columns(act[k], w_down))).astype(bf16))

    grad_down = sum(t_dot(act[k], cot_full[k]) for k in ks).astype(bf16)
    grad_gu = sum(t_dot(raw2[k], d_gu[k]) for k in ks).astype(bf16)

    d_mixed = [dot_t(v, w_out) for v in d_out]
    grad_out = sum(t_dot(mixed[k], d_out[k]) for k in ks).astype(bf16)
    d_conv = [d_mixed[k] * gate_c[k] for k in ks]
    after_last = shifted(d_conv[0][0:2], "seq", -1)
    d_project, inner1 = [], []
    grad_conv = [0.0, 0.0, 0.0]
    for k in ks:
        grad_ext = jnp.concatenate([d_conv[k], after_last if k == chunks - 1 else d_conv[k + 1][0:2]], axis=0)
        d_product = (
            kernel[2] * grad_ext[0:part]
            + kernel[1] * grad_ext[1 : part + 1]
            + kernel[0] * grad_ext[2 : part + 2]
        )
        d_gate_c = d_mixed[k] * conv[k]
        for s in range(3):
            grad_conv[s] = grad_conv[s] + jnp.sum(d_conv[k] * extended[k][s : s + part], axis=0)
        inner1.append(
            total(jnp.sum(2.0 * d_product * product[k] + d_gate_c * gate_c[k], axis=1))[:, None]
        )
        d_project.append(
            (
                jnp.concatenate([d_product * values[k], d_gate_c, d_product * gate_b[k]], axis=1) * inv1[k]
            ).astype(bf16)
        )
    grad_in = sum(t_dot(raw1[k], d_project[k]) for k in ks).astype(bf16)
    grad_tokens = []
    gain1_grad = 0.0
    for k in ks:
        pulled = scatter(columns_t(d_project[k], w_in))
        gain1_grad = gain1_grad + jnp.sum(pulled * x[k], axis=0)
        grad_tokens.append(
            (d_resid[k] + pulled * gain1 - x[k] * (inv1[k] * inv1[k] * inner1[k] * (1.0 / width))).astype(bf16)
        )

    small = jnp.concatenate([jnp.stack(grad_conv), gain1_grad[None], gain2_grad[None]], axis=0)
    small = total(total(small, "dp"), "seq")
    grad_down = absolute(reduce_grad(grad_down), 1)
    gate_sum = absolute(reduce_grad(grad_gu[:, :hidden]), 0)
    up_sum = absolute(reduce_grad(grad_gu[:, hidden:]), 0)
    grad_gate_up = jnp.stack([gate_sum, up_sum], axis=1)
    grad_out = absolute(reduce_grad(grad_out), 1)
    grad_in = absolute(reduce_grad(grad_in), 0).reshape(width, 3, local)
    return (
        jnp.concatenate(result, axis=0),
        jnp.concatenate(grad_tokens, axis=0),
        small[3],
        grad_in,
        small[0:3],
        grad_out,
        small[4],
        grad_gate_up,
        grad_down,
    )


def solution(mesh):
    placed = (
        P(("dp", "seq"), "chan"),
        P("chan"),
        P(None, None, "chan"),
        P(None, "chan"),
        P("chan", None),
        P(),
        P(None, None, "chan"),
        P("chan", None),
        P(("dp", "seq"), "chan"),
    )
    return jax.shard_map(
        shards,
        mesh=mesh,
        in_specs=placed,
        out_specs=(
            P(("dp", "seq"), "chan"),
            P(("dp", "seq"), "chan"),
            P("chan"),
            P(None, None, "chan"),
            P(None, "chan"),
            P("chan", None),
            P("chan"),
            P(None, None, "chan"),
            P("chan", None),
        ),
        check_vma=False,
    )
```
